32 devices in a mesh: slab: 8 (over z, x), pencil: 4 (over y, core).
Axes of the slice: x: 2, y: 2, z: 4, core: 2. Of those that a mesh axis runs over, the one named last changes fastest.
Arguments:
- atom_cell: int32 [3, 262144], P(None, ('slab', 'pencil')), may hold values from 0 to 511, as said below
- charge: float32 [262144], P(('slab', 'pencil')), may hold values from -4 to 4
Outputs:
- potential: float32 [64, 128, 512], P('slab', 'pencil')
- forces: float32 [3, 262144], P(None, ('slab', 'pencil'))
The draws below stay inside these ranges and needn't reach their ends.
Inputs may be any that keep to these rules, and one draw needn't show every extreme that they name: `atom_cell`: the atoms of rows b * 8192 to (b + 1) * 8192 - 1, with b = s * 4 + r, lie in z planes s * 8 to (s + 1) * 8 - 1 and y rows r * 32 to (r + 1) * 32 - 1. Row 0 is at cell (0, 0, 0) and the last row at cell (63, 127, 511).
All inputs are finite; a program needn't handle non-finite values.
Results may differ from the reference program's by a relative error of at most 0.0003.
Values sent between devices are 32-bit elements; how exact they have to be, the bound alone decides.
A program may use at most 128 MiB of HBM per device.

```python
import math
from functools import partial
import jax
import jax.numpy as jnp
from jax import lax

CZ = 8
CY = 32
NX = 512
A_DEV = 8192
LEVELS = 5
RADIUS = 2
F = 32
NZ = 64
NY = 128
TZ = 2
TY = 4
TX = 16
TOPS = 128
ATOMS = 262144


def draw_atom_cell(key, part):
    row_ids = jnp.arange(ATOMS, dtype=jnp.int32)
    block_ids = row_ids // A_DEV
    per_slab = NY // CY
    slab_ids = block_ids // per_slab
    pencil_ids = block_ids % per_slab
    key_z, key_y, key_x = jax.random.split(key, 3)
    cell_z = slab_ids * CZ + jax.random.randint(key_z, (ATOMS,), 0, CZ, dtype=jnp.int32)
    cell_y = pencil_ids * CY + jax.random.randint(key_y, (ATOMS,), 0, CY, dtype=jnp.int32)
    cell_x = jax.random.randint(key_x, (ATOMS,), 0, NX, dtype=jnp.int32)
    first_row = row_ids == 0
    final_row = row_ids == ATOMS - 1
    cell_z = jnp.where(first_row, 0, jnp.where(final_row, NZ - 1, cell_z))
    cell_y = jnp.where(first_row, 0, jnp.where(final_row, NY - 1, cell_y))
    cell_x = jnp.where(first_row, 0, jnp.where(final_row, NX - 1, cell_x))
    return jnp.stack([cell_z, cell_y, cell_x]).astype(jnp.int32)


def draw_charge(key, part):
    values = jnp.clip(jax.random.normal(key, (ATOMS,), jnp.float32), -4.0, 4.0)
    return values


def setup_inputs(seed: int = 0) -> dict:
    streams_of = jax.random.split(jax.random.key(seed), 3)
    return {
        "atom_cell": draw_atom_cell(jax.random.fold_in(streams_of[2], 71), 0),
        "charge": draw_charge(jax.random.fold_in(streams_of[2], 71), 0),
    }


def kernel_weight(step_z, step_y, step_x):
    squared = step_z * step_z + step_y * step_y + step_x * step_x
    return 1.0 / math.sqrt(squared + 0.25) - 1.0 / math.sqrt(squared + 4.0)

def level_weight(scale, step_z, step_y, step_x):
    squared = step_z * step_z + step_y * step_y + step_x * step_x
    return scale * (1.0 / math.sqrt(squared + 1.0) - 1.0 / math.sqrt(squared + 4.0))

def short_field(padded, plane_count, row_count, row_length, radius_cells, weight_of):
    accumulated = jnp.zeros((plane_count, row_count, row_length), jnp.float32)
    for step_z in range(-radius_cells, radius_cells + 1):
        for step_y in range(-radius_cells, radius_cells + 1):
            for step_x in range(-radius_cells, radius_cells + 1):
                corner_z = radius_cells + step_z
                corner_y = radius_cells + step_y
                corner_x = radius_cells + step_x
                accumulated = accumulated + weight_of(step_z, step_y, step_x) * padded[corner_z:corner_z + plane_count, corner_y:corner_y + row_count, corner_x:corner_x + row_length]
    return accumulated

def restrict(grid):
    planes, rows, length = grid.shape
    return grid.reshape(planes // 2, 2, rows // 2, 2, length // 2, 2).sum(axis=(1, 3, 5))

def level_field(grid, weight_of):
    planes, rows, length = grid.shape
    padded = jnp.pad(grid, RADIUS)
    span = 2 * RADIUS + 1

    def one_plane(plane_id):
        window = lax.dynamic_slice_in_dim(padded, plane_id, span, 0)
        return short_field(window, 1, rows, length, RADIUS, weight_of)[0]
    return lax.map(one_plane, jnp.arange(planes, dtype=jnp.int32))

def interp_axis(values, axis, fine_ids, level_count, factor, first_col):
    numerator = jnp.clip(2 * fine_ids + 1 - factor, 0, 2 * factor * (level_count - 1))
    lower_index = jnp.minimum(numerator // (2 * factor), level_count - 2)
    fraction = (numerator - lower_index * 2 * factor).astype(jnp.float32) / (2.0 * factor)
    local_index = (lower_index - first_col).astype(jnp.int32)
    low_values = jnp.take(values, local_index, axis=axis)
    high_values = jnp.take(values, local_index + 1, axis=axis)
    shape = [1, 1, 1]
    shape[axis] = fine_ids.shape[0]
    weight_high = fraction.reshape(shape)
    return (1.0 - weight_high) * low_values + weight_high * high_values

def to_fine(field, counts, factor, plane_ids, line_ids, column_ids, first_z, first_y):
    section = interp_axis(field, 0, plane_ids, counts[0], factor, first_z)
    section = interp_axis(section, 1, line_ids, counts[1], factor, first_y)
    return interp_axis(section, 2, column_ids, counts[2], factor, 0)

def top_coords(cell_ids, top_y, top_x):
    return (cell_ids // (top_y * top_x), cell_ids // top_x % top_y, cell_ids % top_x)

def top_potential(targets, charges_flat, top_z, top_y, top_x, strength):
    sources = jnp.arange(top_z * top_y * top_x, dtype=jnp.int32)
    target_xyz = top_coords(targets, top_y, top_x)
    source_xyz = top_coords(sources, top_y, top_x)
    distance = jnp.ones((targets.shape[0], sources.shape[0]), jnp.float32)
    for component in range(3):
        offset = (target_xyz[component][:, None] - source_xyz[component][None, :]).astype(jnp.float32)
        distance = distance + offset * offset
    kernel = strength / jnp.sqrt(distance)
    return jnp.dot(kernel, charges_flat, precision=lax.Precision.HIGHEST)

def gradient_along(padded, direction, plane_count, row_count, row_length):

    def shifted(offset_cells):
        corner = [2, 2, 2]
        corner[direction] = corner[direction] + offset_cells
        return padded[corner[0]:corner[0] + plane_count, corner[1]:corner[1] + row_count, corner[2]:corner[2] + row_length]
    return (8.0 * (shifted(1) - shifted(-1)) - (shifted(2) - shifted(-2))) / 12.0

def reference(atom_cell, charge):
    cell_index = (atom_cell[0] * NY + atom_cell[1]) * NX + atom_cell[2]
    charge_grid = jax.ops.segment_sum(charge, cell_index, num_segments=NZ * NY * NX).reshape(NZ, NY, NX)
    plane_ids = jnp.arange(NZ, dtype=jnp.int32)
    line_ids = jnp.arange(NY, dtype=jnp.int32)
    column_ids = jnp.arange(NX, dtype=jnp.int32)
    potential = level_field(charge_grid, kernel_weight)
    level_charge = charge_grid
    for level in range(1, LEVELS):
        level_charge = restrict(level_charge)
        field = level_field(level_charge, partial(level_weight, 1.0 / 2 ** level))
        potential = potential + to_fine(field, field.shape, 2 ** level, plane_ids, line_ids, column_ids, 0, 0)
    top_charge = restrict(level_charge)
    charges_flat = top_charge.reshape(TOPS)
    block_rows = math.gcd(TOPS, 512)
    target_blocks = jnp.arange(TOPS, dtype=jnp.int32).reshape(TOPS // block_rows, block_rows)
    strength = 1.0 / F
    top_field = lax.map(lambda targets: top_potential(targets, charges_flat, TZ, TY, TX, strength), target_blocks).reshape(TZ, TY, TX)
    potential = potential + to_fine(top_field, top_field.shape, F, plane_ids, line_ids, column_ids, 0, 0)
    rimmed = jnp.pad(potential, 2)
    gradients = jnp.stack([gradient_along(rimmed, direction, NZ, NY, NX) for direction in range(3)]).reshape(3, NZ * NY * NX)
    forces = -charge[None, :] * jnp.take(gradients, cell_index, axis=1)
    return (potential, forces)
```

```python
from functools import partial
import math

import jax
import jax.numpy as jnp
from jax import lax
from jax.experimental import pallas as pl
from jax.experimental.pallas import tpu as pltpu
from jax.sharding import PartitionSpec as P

CZ = 8
CY = 32
NX = 512
LEVELS = 5
RADIUS = 2
F = 32


def extended(cells, sides, width):
    for axis, dim in sides:
        count = lax.axis_size(axis)
        ends = count - 1
        head = lax.slice_in_dim(cells, 0, width, axis=dim)
        tail = lax.slice_in_dim(cells, cells.shape[dim] - width, cells.shape[dim], axis=dim)
        cells = jnp.concatenate(
            [
                lax.ppermute(tail, axis, [(i, (i + 1) % count) for i in range(ends)]),
                cells,
                lax.ppermute(head, axis, [((i + 1) % count, i) for i in range(ends)]),
            ],
            axis=dim,
        )
    return cells


def kernel_weight(step_z, step_y, step_x):
    squared = step_z * step_z + step_y * step_y + step_x * step_x
    return 1.0 / math.sqrt(squared + 0.25) - 1.0 / math.sqrt(squared + 4.0)


def level_weight(scale, step_z, step_y, step_x):
    squared = step_z * step_z + step_y * step_y + step_x * step_x
    return scale * (1.0 / math.sqrt(squared + 1.0) - 1.0 / math.sqrt(squared + 4.0))


def short_field(padded, plane_count, row_count, row_length, radius_cells, weight_of):
    accumulated = jnp.zeros((plane_count, row_count, row_length), jnp.float32)
    for step_z in range(-radius_cells, radius_cells + 1):
        for step_y in range(-radius_cells, radius_cells + 1):
            for step_x in range(-radius_cells, radius_cells + 1):
                corner_z = radius_cells + step_z
                corner_y = radius_cells + step_y
                corner_x = radius_cells + step_x
                accumulated = (
                    accumulated
                    + weight_of(step_z, step_y, step_x)
                    * padded[
                        corner_z : corner_z + plane_count,
                        corner_y : corner_y + row_count,
                        corner_x : corner_x + row_length,
                    ]
                )
    return accumulated


def restrict(grid):
    planes, rows, length = grid.shape
    return grid.reshape(planes // 2, 2, rows // 2, 2, length // 2, 2).sum(axis=(1, 3, 5))


def restrict_plane(plane):
    rows, length = plane.shape
    return plane.reshape(rows // 2, 2, length // 2, 2).sum(axis=(1, 3))


def interp_matrix(fine_ids, level_count, factor, first_col, width):
    numerator = jnp.clip(2 * fine_ids + 1 - factor, 0, 2 * factor * (level_count - 1))
    lower_index = jnp.minimum(numerator // (2 * factor), level_count - 2)
    fraction = (numerator - lower_index * 2 * factor).astype(jnp.float32) / (2.0 * factor)
    local_index = lower_index - first_col
    columns = jnp.arange(width, dtype=jnp.int32)
    low_part = jnp.where(columns[None, :] == local_index[:, None], 1.0 - fraction[:, None], 0.0)
    high_part = jnp.where(columns[None, :] == local_index[:, None] + 1, fraction[:, None], 0.0)
    return low_part + high_part


def to_fine(field, counts, factor, plane_ids, line_ids, column_ids, first_z, first_y):
    width_z, width_y, width_x = field.shape
    along_z = interp_matrix(plane_ids, counts[0], factor, first_z, width_z)
    along_y = interp_matrix(line_ids, counts[1], factor, first_y, width_y)
    along_x = interp_matrix(column_ids, counts[2], factor, 0, width_x)
    section = jnp.einsum("fa,abc->fbc", along_z, field, precision=lax.Precision.HIGHEST)
    section = jnp.einsum("fb,abc->afc", along_y, section, precision=lax.Precision.HIGHEST)
    return jnp.einsum("fc,abc->abf", along_x, section, precision=lax.Precision.HIGHEST)


def top_coords(cell_ids, top_y, top_x):
    return (cell_ids // (top_y * top_x), cell_ids // top_x % top_y, cell_ids % top_x)


def top_potential(targets, charges_flat, top_z, top_y, top_x, strength):
    sources = jnp.arange(top_z * top_y * top_x, dtype=jnp.int32)
    target_xyz = top_coords(targets, top_y, top_x)
    source_xyz = top_coords(sources, top_y, top_x)
    distance = jnp.ones((targets.shape[0], sources.shape[0]), jnp.float32)
    for component in range(3):
        offset = (target_xyz[component][:, None] - source_xyz[component][None, :]).astype(
            jnp.float32
        )
        distance = distance + offset * offset
    kernel = strength / jnp.sqrt(distance)
    return jnp.dot(kernel, charges_flat, precision=lax.Precision.HIGHEST)


def gradient_along(padded, direction, plane_count, row_count, row_length):

    def shifted(offset_cells):
        corner = [2, 2, 2]
        corner[direction] = corner[direction] + offset_cells
        return padded[
            corner[0] : corner[0] + plane_count,
            corner[1] : corner[1] + row_count,
            corner[2] : corner[2] + row_length,
        ]

    return (8.0 * (shifted(1) - shifted(-1)) - (shifted(2) - shifted(-2))) / 12.0


CHUNK = 1024


def split_two(values):
    high = values.astype(jnp.bfloat16)
    return high, (values - high.astype(jnp.float32)).astype(jnp.bfloat16)


def local_rows(cell_ref, start, width):
    z0 = lax.axis_index("slab") * CZ
    y0 = lax.axis_index("pencil") * CY
    plane = cell_ref[0:1, pl.ds(start, width)] - z0
    line = cell_ref[1:2, pl.ds(start, width)] - y0
    return plane * CY + line, cell_ref[2:3, pl.ds(start, width)]


def deposit_kernel(cell_ref, charge_ref, grid_ref):
    atoms = cell_ref.shape[1]
    width = math.gcd(atoms, CHUNK)
    rows_total = CZ * CY
    grid_ref[...] = jnp.zeros_like(grid_ref)

    @pl.loop(0, atoms // width)
    def _(step):
        start = pl.multiple_of(step * width, width)
        rows, columns = local_rows(cell_ref, start, width)
        charges = charge_ref[:, pl.ds(start, width)]
        high = charges.astype(jnp.bfloat16).astype(jnp.float32)
        low = charges - high
        at_row = lax.broadcasted_iota(jnp.int32, (rows_total, width), 0) == rows
        at_column = lax.broadcasted_iota(jnp.int32, (NX, width), 0) == columns
        table = jnp.where(at_column, 1.0, 0.0).astype(jnp.bfloat16)
        stacked = jnp.concatenate(
            [
                jnp.where(at_row, high, 0.0).astype(jnp.bfloat16),
                jnp.where(at_row, low, 0.0).astype(jnp.bfloat16),
            ],
            axis=0,
        )
        added = lax.dot_general(
            stacked, table, (((1,), (1,)), ((), ())), preferred_element_type=jnp.float32
        )
        grid_ref[...] += added[:rows_total] + added[rows_total:]


def deposit_call(atom_cell, charge):
    return pl.pallas_call(
        deposit_kernel,
        out_shape=jax.ShapeDtypeStruct((CZ * CY, NX), jnp.float32),
        compiler_params=pltpu.CompilerParams(vmem_limit_bytes=48 * 2**20),
    )(atom_cell, charge.reshape(1, -1))


def pick_forces(cell_ref, charge_ref, high_ref, low_ref, force_ref):
    atoms = cell_ref.shape[1]
    width = math.gcd(atoms, 512)
    rows_total = CZ * CY

    @pl.loop(0, atoms // width)
    def _(step):
        start = pl.multiple_of(step * width, width)
        rows, columns = local_rows(cell_ref, start, width)
        charges = charge_ref[:, pl.ds(start, width)]
        at_row = lax.broadcasted_iota(jnp.int32, (rows_total, width), 0) == rows
        at_column = lax.broadcasted_iota(jnp.int32, (NX, width), 0) == columns
        table = jnp.where(at_column, 1.0, 0.0).astype(jnp.bfloat16)
        for direction in range(3):
            part = pl.ds(direction * rows_total, rows_total)
            at_cell = jnp.dot(high_ref[part, :], table, preferred_element_type=jnp.float32)
            at_cell += jnp.dot(low_ref[part, :], table, preferred_element_type=jnp.float32)
            chosen = jnp.sum(jnp.where(at_row, at_cell, 0.0), axis=0, keepdims=True)
            force_ref[direction : direction + 1, pl.ds(start, width)] = -charges * chosen


def pick_kernel(cell_ref, charge_ref, grad_ref, force_ref, high_ref, low_ref):
    high, low = split_two(grad_ref[...])
    high_ref[...] = high
    low_ref[...] = low
    pick_forces(cell_ref, charge_ref, high_ref, low_ref, force_ref)


def pick_call(atom_cell, charge, gradients):
    rows = gradients.shape[0]
    return pl.pallas_call(
        pick_kernel,
        out_shape=jax.ShapeDtypeStruct(atom_cell.shape, jnp.float32),
        scratch_shapes=[pltpu.VMEM((rows, NX), jnp.bfloat16)] * 2,
        compiler_params=pltpu.CompilerParams(vmem_limit_bytes=48 * 2**20),
    )(atom_cell, charge.reshape(1, -1), gradients)


def body(atom_cell, charge):
    slab_pos = lax.axis_index("slab")
    pencil_pos = lax.axis_index("pencil")
    slabs = lax.axis_size("slab")
    pencils = lax.axis_size("pencil")
    charge_grid = deposit_call(atom_cell, charge)
    charge_grid = charge_grid.reshape(CZ, CY, NX)
    plane_ids = slab_pos * CZ + jnp.arange(CZ, dtype=jnp.int32)
    line_ids = pencil_pos * CY + jnp.arange(CY, dtype=jnp.int32)
    column_ids = jnp.arange(NX, dtype=jnp.int32)
    plane_level = CZ.bit_length() - 1
    rimmed = extended(charge_grid, (("slab", 0), ("pencil", 1)), RADIUS)
    padded = jnp.pad(rimmed, ((0, 0), (0, 0), (RADIUS, RADIUS)))
    potential = short_field(padded, CZ, CY, NX, RADIUS, kernel_weight)
    level_charge = charge_grid
    for level in range(1, plane_level):
        level_charge = restrict(level_charge)
        level_z, level_y, level_x = level_charge.shape
        cycle = extended(level_charge, (("slab", 0), ("pencil", 1)), RADIUS)
        cycle = jnp.pad(cycle, ((0, 0), (0, 0), (RADIUS, RADIUS)))
        field = short_field(
            cycle, level_z, level_y, level_x, RADIUS, partial(level_weight, 1.0 / 2**level)
        )
        framed = extended(field, (("slab", 0), ("pencil", 1)), 1)
        counts = (level_z * slabs, level_y * pencils, level_x)
        potential = potential + to_fine(
            framed,
            counts,
            2**level,
            plane_ids,
            line_ids,
            column_ids,
            slab_pos * level_z - 1,
            pencil_pos * level_y - 1,
        )
    own_plane = restrict(level_charge)[0]
    pieces = [own_plane]
    partial_plane = own_plane
    for level_bit in range(LEVELS - plane_level):
        partial_plane = restrict_plane(partial_plane)
        pieces.append(partial_plane)
    packed = jnp.concatenate([piece.reshape(1, -1) for piece in pieces], axis=1)
    gathered = lax.all_gather(packed, ("slab", "pencil"), axis=0, tiled=True)
    coarse = []
    offset = 0
    for step, piece in enumerate(pieces):
        rows, length = piece.shape
        group = 2**step
        block = gathered[:, offset : offset + rows * length].reshape(
            slabs // group, group, pencils, rows, length
        )
        grid = block.sum(axis=1)
        coarse.append(grid.reshape(slabs // group, pencils * rows, length))
        offset = offset + rows * length
    for step in range(LEVELS - plane_level):
        level = plane_level + step
        grid = coarse[step]
        level_z, level_y, level_x = grid.shape
        field = short_field(
            jnp.pad(grid, RADIUS),
            level_z,
            level_y,
            level_x,
            RADIUS,
            partial(level_weight, 1.0 / 2**level),
        )
        potential = potential + to_fine(
            field, field.shape, 2**level, plane_ids, line_ids, column_ids, 0, 0
        )
    top_grid = coarse[-1]
    top_z, top_y, top_x = top_grid.shape
    charges_flat = top_grid.reshape(top_z * top_y * top_x)
    top_total = top_z * top_y * top_x
    strength = 1.0 / F
    block_rows = math.gcd(top_total, 512)
    target_blocks = jnp.arange(top_total, dtype=jnp.int32).reshape(
        top_total // block_rows, block_rows
    )
    top_field = lax.map(
        lambda targets: top_potential(targets, charges_flat, top_z, top_y, top_x, strength),
        target_blocks,
    )
    top_field = top_field.reshape(top_z, top_y, top_x)
    potential = potential + to_fine(
        top_field, top_field.shape, F, plane_ids, line_ids, column_ids, 0, 0
    )
    rimmed_field = extended(potential, (("slab", 0), ("pencil", 1)), 2)
    padded_field = jnp.pad(rimmed_field, ((0, 0), (0, 0), (2, 2)))
    gradients = jnp.stack(
        [gradient_along(padded_field, direction, CZ, CY, NX) for direction in range(3)]
    ).reshape(3 * CZ * CY, NX)
    forces = pick_call(atom_cell, charge, gradients)
    return (potential, forces)


def solution(mesh):
    return jax.shard_map(
        body,
        mesh=mesh,
        in_specs=(P(None, ("slab", "pencil")), P(("slab", "pencil"))),
        out_specs=(P("slab", "pencil", None), P(None, ("slab", "pencil"))),
        check_vma=False,
    )
```

```python
import functools
import math

import jax
import jax.numpy as jnp
import numpy as np
from jax import lax
from jax.experimental import pallas as pl
from jax.experimental.pallas import tpu as pltpu
from jax.sharding import PartitionSpec as P

CZ = 8
CY = 32
NX = 512
F = 32
ROWS = CZ * CY
CHUNK = 1024
MESH = pl.DeviceIdType.MESH
HIGHEST = lax.Precision.HIGHEST
VMEM = pl.BlockSpec(memory_space=pltpu.VMEM)
SQUARES = (0, 1, 2, 4, 5, 8)


def iota(shape, dim):
    return lax.broadcasted_iota(jnp.int32, shape, dim)


def near_weight(squared):
    return 1.0 / math.sqrt(squared + 0.25) - 1.0 / math.sqrt(squared + 4.0)


def level_weight(level, squared):
    return (1.0 / math.sqrt(squared + 1.0) - 1.0 / math.sqrt(squared + 4.0)) / 2**level


def dot32(left, right):
    return jnp.dot(left, right, precision=HIGHEST, preferred_element_type=jnp.float32)


def split_two(values):
    high = values.astype(jnp.bfloat16)
    return high, (values - high.astype(jnp.float32)).astype(jnp.bfloat16)


def local_rows(cell_ref, start, width):
    z0 = lax.axis_index("slab") * CZ
    y0 = lax.axis_index("pencil") * CY
    plane = cell_ref[0:1, pl.ds(start, width)] - z0
    line = cell_ref[1:2, pl.ds(start, width)] - y0
    return plane * CY + line, cell_ref[2:3, pl.ds(start, width)]


def halve_rows(rows_out, rows_in, line_bits):
    out_row = iota((rows_out, rows_in), 0)
    in_row = iota((rows_out, rows_in), 1)
    plane = in_row >> (line_bits + 1)
    line = (in_row & (2**line_bits - 1)) >> 1
    return jnp.where((plane << (line_bits - 1)) + line == out_row, 1.0, 0.0)


def halve_columns(columns_in, columns_out):
    return jnp.where(
        iota((columns_in, columns_out), 0) >> 1 == iota((columns_in, columns_out), 1), 1.0, 0.0
    )


def deposit_kernel(cell_ref, charge_ref, grid_ref, one_ref, two_ref, three_ref, total_ref):
    atoms = cell_ref.shape[1]
    width = math.gcd(atoms, CHUNK)
    total_ref[...] = jnp.zeros_like(total_ref)

    @pl.loop(0, atoms // width)
    def _(step):
        start = pl.multiple_of(step * width, width)
        rows, columns = local_rows(cell_ref, start, width)
        charges = charge_ref[:, pl.ds(start, width)]
        high = charges.astype(jnp.bfloat16).astype(jnp.float32)
        low = charges - high
        at_row = iota((ROWS, width), 0) == rows
        table = jnp.where(iota((NX, width), 0) == columns, 1.0, 0.0).astype(jnp.bfloat16)
        stacked = jnp.concatenate(
            [
                jnp.where(at_row, high, 0.0).astype(jnp.bfloat16),
                jnp.where(at_row, low, 0.0).astype(jnp.bfloat16),
            ],
            axis=0,
        )
        added = lax.dot_general(
            stacked, table, (((1,), (1,)), ((), ())), preferred_element_type=jnp.float32
        )
        total_ref[...] += added[:ROWS] + added[ROWS:]

    grid = total_ref[...]
    grid_ref[...] = grid.reshape(CZ, CY, NX)
    one = dot32(dot32(halve_rows(ROWS // 4, ROWS, 5), grid), halve_columns(NX, NX // 2))
    one_ref[...] = one.reshape(CZ // 2, CY // 2, NX // 2)
    two = dot32(
        dot32(halve_rows(ROWS // 16, ROWS // 4, 4), one), halve_columns(NX // 2, NX // 4)
    )
    two_ref[...] = two.reshape(CZ // 4, CY // 4, NX // 4)
    three_ref[...] = dot32(
        dot32(halve_rows(8, ROWS // 16, 3), two), halve_columns(NX // 4, NX // 4)
    )


def deposit_call(atom_cell, charge):
    shapes = ((CZ, CY, NX), (CZ // 2, CY // 2, NX // 2), (CZ // 4, CY // 4, NX // 4), (8, 128))
    return pl.pallas_call(
        deposit_kernel,
        out_shape=[jax.ShapeDtypeStruct(shape, jnp.float32) for shape in shapes],
        in_specs=[VMEM] * 2,
        out_specs=[VMEM] * 4,
        scratch_shapes=[pltpu.VMEM((ROWS, NX), jnp.float32)],
        compiler_params=pltpu.CompilerParams(vmem_limit_bytes=48 * 2**20),
    )(atom_cell, charge.reshape(1, -1))


def window(level, dz, dy):
    if level == 0:
        z = {1: (4, 0, 4), -1: (0, 12, 4), 0: (0, 4, 8)}[dz]
        y = {1: (24, 0, 8), -1: (0, 40, 8), 0: (0, 8, 32)}[dy]
    elif level == 1:
        z = {1: (0, 0, 4), -1: (0, 8, 4), 0: (0, 4, 4)}[dz]
        y = {1: (8, 0, 8), -1: (0, 24, 8), 0: (0, 8, 16)}[dy]
    else:
        z = (0, 4 - 2 * dz, 2)
        y = (0, 8 - 8 * dy, 8)
    return z, y


def exchange_kernel(
    slabs, pencils, zero, one, two, three, wide0, wide1, wide2, wide3, send, recv, send3, recv3
):
    slab = lax.axis_index("slab")
    pencil = lax.axis_index("pencil")
    devices = slabs * pencils
    me = slab * pencils + pencil
    for ref in (wide0, wide1, wide2):
        ref[...] = jnp.zeros_like(ref)
    wide0[4:12, 8:40, :] = zero[...]
    wide1[4:8, 8:24, :] = one[...]
    wide2[4:6, 8:16, :] = two[...]
    wide3[pl.ds(me, 1)] = three[...][None]

    def place(step):
        other = lax.rem(me + step, devices)
        return (other // pencils, lax.rem(other, pencils))

    barrier = pltpu.get_barrier_semaphore()

    @pl.loop(1, devices)
    def _(step):
        pl.semaphore_signal(barrier, inc=1, device_id=place(step), device_id_type=MESH)

    pl.semaphore_wait(barrier, devices - 1)

    offsets = [(0, dz, dy) for dz in (-1, 0, 1) for dy in (-1, 0, 1) if dz or dy]
    offsets += [(1, dz, dy) for dz in (-1, 0, 1) for dy in (-1, 0, 1) if dz or dy]
    offsets += [(2, dz, dy) for dz in range(-2, 3) for dy in (-1, 0, 1) if dz or dy]
    sources = (zero, one, two)
    targets = (wide0, wide1, wide2)

    def inside(dz, dy):
        z = slab + dz
        y = pencil + dy
        return (z >= 0) & (z < slabs) & (y >= 0) & (y < pencils)

    def copy_of(index, device):
        level, dz, dy = offsets[index]
        (zs, zd, zn), (ys, yd, yn) = window(level, dz, dy)
        return pltpu.make_async_remote_copy(
            src_ref=sources[level].at[pl.ds(zs, zn), pl.ds(ys, yn), :],
            dst_ref=targets[level].at[pl.ds(zd, zn), pl.ds(yd, yn), :],
            send_sem=send.at[index],
            recv_sem=recv.at[index],
            device_id=device,
            device_id_type=MESH,
        )

    def top_copy(step, slot):
        return pltpu.make_async_remote_copy(
            src_ref=three,
            dst_ref=wide3.at[slot],
            send_sem=send3.at[step],
            recv_sem=recv3.at[step],
            device_id=place(step),
            device_id_type=MESH,
        )

    for index, (level, dz, dy) in enumerate(offsets):

        @pl.when(inside(dz, dy))
        def _():
            copy_of(index, (slab + dz, pencil + dy)).start()

    @pl.loop(1, devices)
    def _(step):
        top_copy(step, me).start()

    @pl.loop(1, devices)
    def _(step):
        copy = top_copy(step, lax.rem(me + devices - step, devices))
        copy.wait_send()
        copy.wait_recv()

    for index, (level, dz, dy) in enumerate(offsets):

        @pl.when(inside(-dz, -dy))
        def _():
            copy_of(index, (slab - dz, pencil - dy)).wait_recv()

        @pl.when(inside(dz, dy))
        def _():
            copy_of(index, (slab + dz, pencil + dy)).wait_send()


def exchange_call(slabs, pencils, parts):
    devices = slabs * pencils
    shapes = ((16, 48, NX), (12, 32, NX // 2), (10, 32, NX // 4), (devices, 8, 128))
    return pl.pallas_call(
        functools.partial(exchange_kernel, slabs, pencils),
        out_shape=[jax.ShapeDtypeStruct(shape, jnp.float32) for shape in shapes],
        in_specs=[VMEM] * 4,
        out_specs=[VMEM] * 4,
        scratch_shapes=[
            pltpu.SemaphoreType.DMA((30,)),
            pltpu.SemaphoreType.DMA((30,)),
            pltpu.SemaphoreType.DMA((devices,)),
            pltpu.SemaphoreType.DMA((devices,)),
        ],
        compiler_params=pltpu.CompilerParams(
            collective_id=0, has_side_effects=True, vmem_limit_bytes=48 * 2**20
        ),
    )(*parts)


def shift_x(values, step):
    width = values.shape[-1]
    axis = values.ndim - 1
    column = iota(values.shape, axis)
    moved = pltpu.roll(values, (-step) % width, axis)
    return jnp.where((column + step >= 0) & (column + step < width), moved, 0.0)


def pair_x(values, step):
    return shift_x(values, step) + shift_x(values, -step)


def hat(fine, cell, factor, count):
    bits = factor.bit_length()
    numerator = jnp.clip(2 * fine + 1 - factor, 0, 2 * factor * (count - 1))
    lower = jnp.minimum(numerator >> bits, count - 2)
    fraction = (numerator - (lower << bits)).astype(jnp.float32) * (0.5 / factor)
    return jnp.where(
        cell == lower, 1.0 - fraction, jnp.where(cell == lower + 1, fraction, 0.0)
    )


def window_stencil(level, planes_in, planes_out, lines, shift):
    blocks = []
    dz = np.arange(planes_in)[None, :] - np.arange(planes_out)[:, None] + shift
    dy = np.arange(lines)[None, :] - np.arange(lines)[:, None]
    dz = dz[:, None, :, None]
    dy = dy[None, :, None, :]
    near = (np.abs(dz) <= 2) & (np.abs(dy) <= 2)
    for c in range(3):
        squared = (dz * dz + dy * dy + c * c).astype(np.float64)
        weight = (1.0 / np.sqrt(squared + 1.0) - 1.0 / np.sqrt(squared + 4.0)) / 2**level
        weight = np.where(near, weight, 0.0)
        blocks.append(weight.reshape(planes_out * lines, planes_in * lines))
    return np.concatenate(blocks, axis=1).astype(np.float32)


def field_kernel(
    slabs,
    pencils,
    cell_ref,
    charge_ref,
    wide0,
    wide1,
    wide2,
    wide3,
    stencil1,
    stencil2,
    pot_ref,
    force_ref,
    sums,
    wide_pot,
    field1,
    field2,
    field3,
    along_x,
    high_ref,
    low_ref,
):
    slab = lax.axis_index("slab")
    pencil = lax.axis_index("pencil")
    pencil_bits = pencils.bit_length() - 1

    grid1 = wide1[...].reshape(12 * 32, NX // 2)
    field1[...] = dot32(
        stencil1[...], jnp.concatenate([grid1, pair_x(grid1, 1), pair_x(grid1, 2)], axis=0)
    )
    grid2 = wide2[...].reshape(10 * 32, NX // 4)
    field2[...] = dot32(
        stencil2[...], jnp.concatenate([grid2, pair_x(grid2, 1), pair_x(grid2, 2)], axis=0)
    )
    rows3 = slabs * pencils * 8
    grid3 = wide3[...].reshape(rows3, 128)
    coarse = []
    first_row = 0
    first_lane = 0
    for level in (3, 4, 5):
        down = level - 3
        line_bits = pencil_bits + 2 - down
        lines = 2**line_bits
        planes = slabs >> down
        count = planes * lines
        length = NX >> level
        shape = (count, rows3)
        out_row = iota(shape, 0)
        in_row = iota(shape, 1)
        in_plane = in_row >> (3 + pencil_bits)
        in_line = (((in_row >> 3) & (pencils - 1)) << 2) + (in_row & 7)
        cell = ((in_plane >> down) << line_bits) + (in_line >> down)
        chosen = jnp.where((cell == out_row) & ((in_row & 7) < 4), 1.0, 0.0)
        charges = dot32(chosen, grid3)
        reach = 3 if level < 5 else length
        source = iota((128, 128), 0) >> down
        column = iota((128, 128), 1) - first_lane
        valid = (column >= 0) & (column < length)
        pairs = jnp.concatenate(
            [
                jnp.where(valid & (jnp.abs(source - column) == c), 1.0, 0.0)
                for c in range(reach)
            ],
            axis=1,
        )
        moved = dot32(charges, pairs)
        stacked = jnp.concatenate(
            [moved[:, c * 128 : (c + 1) * 128] for c in range(reach)], axis=0
        )
        blocks = []
        for c in range(reach):
            shape = (4 * lines, count)
            dz = (iota(shape, 1) >> line_bits) - (iota(shape, 0) >> line_bits)
            dz = dz - ((slab >> down) - 1)
            dy = (iota(shape, 1) & (lines - 1)) - (iota(shape, 0) & (lines - 1))
            squared = dz * dz + dy * dy
            if level < 5:
                weight = jnp.zeros(shape, jnp.float32)
                for value in SQUARES:
                    weight = jnp.where(
                        squared == value, level_weight(level, value + c * c), weight
                    )
                weight = jnp.where((jnp.abs(dz) <= 2) & (jnp.abs(dy) <= 2), weight, 0.0)
            else:
                weight = (1.0 / F) / jnp.sqrt((squared + (c * c + 1)).astype(jnp.float32))
            blocks.append(dot32(weight, stacked[c * count : (c + 1) * count]))
        field3[first_row : first_row + 4 * lines, :] = sum(blocks[1:], blocks[0])
        first_row = first_row + 4 * lines
        first_lane = first_lane + length

    lane = 0
    for level in range(1, 6):
        length = NX >> level
        rows = length if level < 5 else NX - lane
        weights = hat(iota((rows, NX), 1), iota((rows, NX), 0), 2**level, length)
        weights = jnp.where(iota((rows, NX), 0) < length, weights, 0.0)
        along_x[lane : lane + rows, :] = weights.astype(jnp.bfloat16)
        lane = lane + rows

    @pl.loop(0, 4)
    def _(step):

        def along_zy(level, planes, lines, plane0, line0):
            shape = (3, 48, planes * lines)
            bits = lines.bit_length() - 1
            fine_z = CZ * slab - 2 + 3 * step + iota(shape, 0)
            fine_y = CY * pencil - 8 + iota(shape, 1)
            plane = plane0 + (iota(shape, 2) >> bits)
            line = line0 + (iota(shape, 2) & (lines - 1))
            weights = hat(fine_z, plane, 2**level, (slabs * CZ) >> level) * hat(
                fine_y, line, 2**level, (pencils * CY) >> level
            )
            return weights.reshape(3 * 48, planes * lines)

        parts = [
            dot32(along_zy(1, 8, 32, 4 * slab - 2, 16 * pencil - 8), field1[...]),
            dot32(along_zy(2, 4, 32, 2 * slab - 1, 8 * pencil - 8), field2[...]),
        ]
        first_row = 0
        last = jnp.zeros((3 * 48, 128), jnp.float32)
        for level in (3, 4, 5):
            lines = (pencils * CY) >> level
            weights = along_zy(level, 4, lines, (slab >> (level - 3)) - 1, 0)
            last = last + dot32(weights, field3[first_row : first_row + 4 * lines, :])
            first_row = first_row + 4 * lines
        parts.append(last)
        high, low = split_two(jnp.concatenate(parts, axis=1))
        fine = jnp.dot(high, along_x[...], preferred_element_type=jnp.float32)
        fine += jnp.dot(low, along_x[...], preferred_element_type=jnp.float32)
        wide_pot[pl.ds(4 + 3 * step, 3)] = fine.reshape(3, 48, NX)

    for edge in (0, 1, 2, 3, 16, 17, 18, 19):
        wide_pot[edge] = jnp.zeros((48, NX), jnp.float32)

    @pl.loop(0, 16)
    def _(plane):
        values = wide0[plane]
        sums[0] = values
        sums[1] = pair_x(values, 1)
        sums[2] = pair_x(values, 2)
        for block in range(NX // 128):
            lanes = pl.ds(block * 128, 128)
            table = {}
            for c in range(3):
                part = sums[c, :, lanes]
                table[0, c] = part
                for b in (1, 2):
                    table[b, c] = pltpu.roll(part, b, 0) + pltpu.roll(part, 48 - b, 0)
            groups = {
                0: table[0, 0],
                1: table[0, 1] + table[1, 0],
                2: table[1, 1],
                4: table[0, 2] + table[2, 0],
                5: table[1, 2] + table[2, 1],
                8: table[2, 2],
            }
            for a in range(3):
                total = sum(near_weight(a * a + k) * groups[k] for k in SQUARES)
                for target in {a, -a}:
                    wide_pot[plane + 2 + target, :, lanes] += total

    @pl.loop(0, 12)
    def _(plane):
        shape = (48, NX)
        row = CY * pencil - 8 + iota(shape, 0)
        whole_plane = CZ * slab - 2 + plane + jnp.zeros(shape, jnp.int32)
        valid = (row >= 0) & (row < pencils * CY)
        valid = valid & (whole_plane >= 0) & (whole_plane < slabs * CZ)
        wide_pot[plane + 4] = jnp.where(valid, wide_pot[plane + 4], 0.0)

    def slope(after1, before1, after2, before2):
        return (8.0 * (after1 - before1) - (after2 - before2)) * (1.0 / 12.0)

    @pl.loop(0, CZ)
    def _(plane):
        middle = wide_pot[plane + 6]
        own = middle[8:40]
        pot_ref[plane] = own
        at = [wide_pot[plane + 6 + k, 8:40, :] for k in (1, -1, 2, -2)]
        across = [pltpu.roll(middle, (-k) % 48, 0)[8:40] for k in (1, -1, 2, -2)]
        along = [shift_x(own, k) for k in (1, -1, 2, -2)]
        for direction, four in enumerate((at, across, along)):
            high, low = split_two(slope(*four))
            start = pl.multiple_of(direction * ROWS + plane * CY, CY)
            high_ref[pl.ds(start, CY), :] = high
            low_ref[pl.ds(start, CY), :] = low

    atoms = cell_ref.shape[1]
    width = math.gcd(atoms, 512)

    @pl.loop(0, atoms // width)
    def _(step):
        start = pl.multiple_of(step * width, width)
        rows, columns = local_rows(cell_ref, start, width)
        charges = charge_ref[:, pl.ds(start, width)]
        at_row = iota((ROWS, width), 0) == rows
        table = jnp.where(iota((NX, width), 0) == columns, 1.0, 0.0).astype(jnp.bfloat16)
        for direction in range(3):
            part = pl.ds(direction * ROWS, ROWS)
            at_cell = jnp.dot(high_ref[part, :], table, preferred_element_type=jnp.float32)
            at_cell += jnp.dot(low_ref[part, :], table, preferred_element_type=jnp.float32)
            chosen = jnp.sum(jnp.where(at_row, at_cell, 0.0), axis=0, keepdims=True)
            force_ref[direction : direction + 1, pl.ds(start, width)] = -charges * chosen


def field_call(slabs, pencils, atom_cell, charge, wide):
    stencil1 = window_stencil(1, 12, 8, 32, -2)
    stencil2 = window_stencil(2, 10, 4, 32, -3)
    field3_rows = sum(4 * ((pencils * CY) >> level) for level in (3, 4, 5))
    return pl.pallas_call(
        functools.partial(field_kernel, slabs, pencils),
        out_shape=[
            jax.ShapeDtypeStruct((CZ, CY, NX), jnp.float32),
            jax.ShapeDtypeStruct(atom_cell.shape, jnp.float32),
        ],
        in_specs=[VMEM] * 8,
        out_specs=[VMEM] * 2,
        scratch_shapes=[
            pltpu.VMEM((3, 48, NX), jnp.float32),
            pltpu.VMEM((20, 48, NX), jnp.float32),
            pltpu.VMEM((8 * 32, NX // 2), jnp.float32),
            pltpu.VMEM((4 * 32, NX // 4), jnp.float32),
            pltpu.VMEM((field3_rows, 128), jnp.float32),
            pltpu.VMEM((NX, NX), jnp.bfloat16),
            pltpu.VMEM((3 * ROWS, NX), jnp.bfloat16),
            pltpu.VMEM((3 * ROWS, NX), jnp.bfloat16),
        ],
        compiler_params=pltpu.CompilerParams(vmem_limit_bytes=56 * 2**20),
    )(
        atom_cell,
        charge.reshape(1, -1),
        *wide,
        jnp.asarray(stencil1),
        jnp.asarray(stencil2),
    )


def solution(mesh):
    slabs = mesh.shape["slab"]
    pencils = mesh.shape["pencil"]

    def body(atom_cell, charge):
        parts = deposit_call(atom_cell, charge)
        wide = exchange_call(slabs, pencils, parts)
        potential, forces = field_call(slabs, pencils, atom_cell, charge, wide)
        return (potential, forces)

    return jax.shard_map(
        body,
        mesh=mesh,
        in_specs=(P(None, ("slab", "pencil")), P(("slab", "pencil"))),
        out_specs=(P("slab", "pencil", None), P(None, ("slab", "pencil"))),
        check_vma=False,
    )
```

```python
import functools
import math

import jax
import jax.numpy as jnp
import numpy as np
from jax import lax
from jax.experimental import pallas as pl
from jax.experimental.pallas import tpu as pltpu
from jax.sharding import PartitionSpec as P

CZ = 8
CY = 32
NX = 512
F = 32
ROWS = CZ * CY
CHUNK = 1024
MESH = pl.DeviceIdType.MESH
HIGHEST = lax.Precision.HIGHEST
VMEM = pl.BlockSpec(memory_space=pltpu.VMEM)
SQUARES = (0, 1, 2, 4, 5, 8)


def iota(shape, dim):
    return lax.broadcasted_iota(jnp.int32, shape, dim)


def near_weight(squared):
    return 1.0 / math.sqrt(squared + 0.25) - 1.0 / math.sqrt(squared + 4.0)


def level_weight(level, squared):
    return (1.0 / math.sqrt(squared + 1.0) - 1.0 / math.sqrt(squared + 4.0)) / 2**level


def dot32(left, right):
    return jnp.dot(left, right, precision=HIGHEST, preferred_element_type=jnp.float32)


def split_two(values):
    high = values.astype(jnp.bfloat16)
    return high, (values - high.astype(jnp.float32)).astype(jnp.bfloat16)


def local_rows(cell_ref, start, width):
    z0 = lax.axis_index("slab") * CZ
    y0 = lax.axis_index("pencil") * CY
    plane = cell_ref[0:1, pl.ds(start, width)] - z0
    line = cell_ref[1:2, pl.ds(start, width)] - y0
    return plane * CY + line, cell_ref[2:3, pl.ds(start, width)]


def halve_rows(rows_out, rows_in, line_bits):
    out_row = iota((rows_out, rows_in), 0)
    in_row = iota((rows_out, rows_in), 1)
    plane = in_row >> (line_bits + 1)
    line = (in_row & (2**line_bits - 1)) >> 1
    return jnp.where((plane << (line_bits - 1)) + line == out_row, 1.0, 0.0)


def halve_columns(columns_in, columns_out):
    return jnp.where(
        iota((columns_in, columns_out), 0) >> 1 == iota((columns_in, columns_out), 1), 1.0, 0.0
    )


def deposit_kernel(cell_ref, charge_ref, grid_ref, one_ref, two_ref, three_ref, total_ref):
    atoms = cell_ref.shape[1]
    width = math.gcd(atoms, CHUNK)
    total_ref[...] = jnp.zeros_like(total_ref)

    @pl.loop(0, atoms // width)
    def _(step):
        start = pl.multiple_of(step * width, width)
        rows, columns = local_rows(cell_ref, start, width)
        charges = charge_ref[:, pl.ds(start, width)]
        high = charges.astype(jnp.bfloat16).astype(jnp.float32)
        low = charges - high
        at_row = iota((ROWS, width), 0) == rows
        table = jnp.where(iota((NX, width), 0) == columns, 1.0, 0.0).astype(jnp.bfloat16)
        stacked = jnp.concatenate(
            [
                jnp.where(at_row, high, 0.0).astype(jnp.bfloat16),
                jnp.where(at_row, low, 0.0).astype(jnp.bfloat16),
            ],
            axis=0,
        )
        added = lax.dot_general(
            stacked, table, (((1,), (1,)), ((), ())), preferred_element_type=jnp.float32
        )
        total_ref[...] += added[:ROWS] + added[ROWS:]

    grid = total_ref[...]
    grid_ref[...] = grid.reshape(CZ, CY, NX)
    one = dot32(dot32(halve_rows(ROWS // 4, ROWS, 5), grid), halve_columns(NX, NX // 2))
    one_ref[...] = one.reshape(CZ // 2, CY // 2, NX // 2)
    two = dot32(
        dot32(halve_rows(ROWS // 16, ROWS // 4, 4), one), halve_columns(NX // 2, NX // 4)
    )
    two_ref[...] = two.reshape(CZ // 4, CY // 4, NX // 4)
    three_ref[...] = dot32(
        dot32(halve_rows(8, ROWS // 16, 3), two), halve_columns(NX // 4, NX // 4)
    )


def deposit_call(atom_cell, charge):
    shapes = ((CZ, CY, NX), (CZ // 2, CY // 2, NX // 2), (CZ // 4, CY // 4, NX // 4), (8, 128))
    return pl.pallas_call(
        deposit_kernel,
        out_shape=[jax.ShapeDtypeStruct(shape, jnp.float32) for shape in shapes],
        in_specs=[VMEM] * 2,
        out_specs=[VMEM] * 4,
        scratch_shapes=[pltpu.VMEM((ROWS, NX), jnp.float32)],
        compiler_params=pltpu.CompilerParams(vmem_limit_bytes=48 * 2**20),
    )(atom_cell, charge.reshape(1, -1))


def window(level, dz, dy):
    if level == 0:
        z = {1: (4, 0, 4), -1: (0, 12, 4), 0: (0, 0, 16)}[dz]
        y = {1: (32, 0, 8), -1: (8, 40, 8), 0: (0, 8, 32)}[dy]
    elif level == 1:
        z = {1: (0, 0, 4), -1: (0, 8, 4), 0: (0, 0, 12)}[dz]
        y = {1: (16, 0, 8), -1: (8, 24, 8), 0: (0, 8, 16)}[dy]
    else:
        z = (0, 4 - 2 * dz, 2)
        y = (0, 8 - 8 * dy, 8)
    return z, y


def exchange_kernel(
    slabs, pencils, zero, one, two, three, wide0, wide1, wide2, wide3, send, recv, send3, recv3
):
    slab = lax.axis_index("slab")
    pencil = lax.axis_index("pencil")
    devices = slabs * pencils
    me = slab * pencils + pencil
    for ref in (wide0, wide1, wide2):
        ref[...] = jnp.zeros_like(ref)
    wide0[4:12, 8:40, :] = zero[...]
    wide1[4:8, 8:24, :] = one[...]
    wide2[4:6, 8:16, :] = two[...]
    wide3[pl.ds(me, 1)] = three[...][None]

    def place(step):
        other = lax.rem(me + step, devices)
        return (other // pencils, lax.rem(other, pencils))

    barrier = pltpu.get_barrier_semaphore()

    @pl.loop(1, devices)
    def _(step):
        pl.semaphore_signal(barrier, inc=1, device_id=place(step), device_id_type=MESH)

    pl.semaphore_wait(barrier, devices - 1)

    offsets = [(level, dz, 0) for level in (0, 1) for dz in (-1, 1)]
    offsets += [(level, 0, dy) for level in (0, 1) for dy in (-1, 1)]
    offsets += [(2, dz, dy) for dz in range(-2, 3) for dy in (-1, 0, 1) if dz or dy]
    sources = (zero, one, two)
    targets = (wide0, wide1, wide2)

    def inside(dz, dy):
        z = slab + dz
        y = pencil + dy
        return (z >= 0) & (z < slabs) & (y >= 0) & (y < pencils)

    def copy_of(index, device):
        level, dz, dy = offsets[index]
        (zs, zd, zn), (ys, yd, yn) = window(level, dz, dy)
        return pltpu.make_async_remote_copy(
            src_ref=(targets if level < 2 and dy else sources)[level].at[pl.ds(zs, zn), pl.ds(ys, yn), :],
            dst_ref=targets[level].at[pl.ds(zd, zn), pl.ds(yd, yn), :],
            send_sem=send.at[index],
            recv_sem=recv.at[index],
            device_id=device,
            device_id_type=MESH,
        )

    def top_copy(step, slot):
        return pltpu.make_async_remote_copy(
            src_ref=three,
            dst_ref=wide3.at[slot],
            send_sem=send3.at[step],
            recv_sem=recv3.at[step],
            device_id=place(step),
            device_id_type=MESH,
        )

    def start(indices):
        for index in indices:
            level, dz, dy = offsets[index]

            @pl.when(inside(dz, dy))
            def _(index=index, dz=dz, dy=dy):
                copy_of(index, (slab + dz, pencil + dy)).start()

    def finish(indices):
        for index in indices:
            level, dz, dy = offsets[index]

            @pl.when(inside(-dz, -dy))
            def _(index=index, dz=dz, dy=dy):
                copy_of(index, (slab - dz, pencil - dy)).wait_recv()

            @pl.when(inside(dz, dy))
            def _(index=index, dz=dz, dy=dy):
                copy_of(index, (slab + dz, pencil + dy)).wait_send()

    start(range(4))
    start(range(8, len(offsets)))

    @pl.loop(1, devices)
    def _(step):
        top_copy(step, me).start()

    finish(range(4))
    start(range(4, 8))

    @pl.loop(1, devices)
    def _(step):
        copy = top_copy(step, lax.rem(me + devices - step, devices))
        copy.wait_send()
        copy.wait_recv()

    finish(range(4, len(offsets)))


def exchange_call(slabs, pencils, parts):
    devices = slabs * pencils
    shapes = ((16, 48, NX), (12, 32, NX // 2), (10, 32, NX // 4), (devices, 8, 128))
    return pl.pallas_call(
        functools.partial(exchange_kernel, slabs, pencils),
        out_shape=[jax.ShapeDtypeStruct(shape, jnp.float32) for shape in shapes],
        in_specs=[VMEM] * 4,
        out_specs=[VMEM] * 4,
        scratch_shapes=[
            pltpu.SemaphoreType.DMA((22,)),
            pltpu.SemaphoreType.DMA((22,)),
            pltpu.SemaphoreType.DMA((devices,)),
            pltpu.SemaphoreType.DMA((devices,)),
        ],
        compiler_params=pltpu.CompilerParams(
            collective_id=0, has_side_effects=True, vmem_limit_bytes=48 * 2**20
        ),
    )(*parts)


def shift_x(values, step):
    width = values.shape[-1]
    axis = values.ndim - 1
    column = iota(values.shape, axis)
    moved = pltpu.roll(values, (-step) % width, axis)
    return jnp.where((column + step >= 0) & (column + step < width), moved, 0.0)


def pair_x(values, step):
    return shift_x(values, step) + shift_x(values, -step)


def hat(fine, cell, factor, count):
    bits = factor.bit_length()
    numerator = jnp.clip(2 * fine + 1 - factor, 0, 2 * factor * (count - 1))
    lower = jnp.minimum(numerator >> bits, count - 2)
    fraction = (numerator - (lower << bits)).astype(jnp.float32) * (0.5 / factor)
    return jnp.where(
        cell == lower, 1.0 - fraction, jnp.where(cell == lower + 1, fraction, 0.0)
    )


def window_stencil(level, planes_in, planes_out, lines, shift):
    blocks = []
    dz = np.arange(planes_in)[None, :] - np.arange(planes_out)[:, None] + shift
    dy = np.arange(lines)[None, :] - np.arange(lines)[:, None]
    dz = dz[:, None, :, None]
    dy = dy[None, :, None, :]
    near = (np.abs(dz) <= 2) & (np.abs(dy) <= 2)
    for c in range(3):
        squared = (dz * dz + dy * dy + c * c).astype(np.float64)
        weight = (1.0 / np.sqrt(squared + 1.0) - 1.0 / np.sqrt(squared + 4.0)) / 2**level
        weight = np.where(near, weight, 0.0)
        blocks.append(weight.reshape(planes_out * lines, planes_in * lines))
    return np.concatenate(blocks, axis=1).astype(np.float32)


def field_kernel(
    slabs,
    pencils,
    cell_ref,
    charge_ref,
    wide0,
    wide1,
    wide2,
    wide3,
    stencil1,
    stencil2,
    pot_ref,
    force_ref,
    sums,
    wide_pot,
    field1,
    field2,
    field3,
    along_x,
    high_ref,
    low_ref,
):
    slab = lax.axis_index("slab")
    pencil = lax.axis_index("pencil")
    pencil_bits = pencils.bit_length() - 1

    grid1 = wide1[...].reshape(12 * 32, NX // 2)
    field1[...] = dot32(
        stencil1[...], jnp.concatenate([grid1, pair_x(grid1, 1), pair_x(grid1, 2)], axis=0)
    )
    grid2 = wide2[...].reshape(10 * 32, NX // 4)
    field2[...] = dot32(
        stencil2[...], jnp.concatenate([grid2, pair_x(grid2, 1), pair_x(grid2, 2)], axis=0)
    )
    rows3 = slabs * pencils * 8
    grid3 = wide3[...].reshape(rows3, 128)
    coarse = []
    first_row = 0
    first_lane = 0
    for level in (3, 4, 5):
        down = level - 3
        line_bits = pencil_bits + 2 - down
        lines = 2**line_bits
        planes = slabs >> down
        count = planes * lines
        length = NX >> level
        shape = (count, rows3)
        out_row = iota(shape, 0)
        in_row = iota(shape, 1)
        in_plane = in_row >> (3 + pencil_bits)
        in_line = (((in_row >> 3) & (pencils - 1)) << 2) + (in_row & 7)
        cell = ((in_plane >> down) << line_bits) + (in_line >> down)
        chosen = jnp.where((cell == out_row) & ((in_row & 7) < 4), 1.0, 0.0)
        charges = dot32(chosen, grid3)
        reach = 3 if level < 5 else length
        source = iota((128, 128), 0) >> down
        column = iota((128, 128), 1) - first_lane
        valid = (column >= 0) & (column < length)
        pairs = jnp.concatenate(
            [
                jnp.where(valid & (jnp.abs(source - column) == c), 1.0, 0.0)
                for c in range(reach)
            ],
            axis=1,
        )
        moved = dot32(charges, pairs)
        stacked = jnp.concatenate(
            [moved[:, c * 128 : (c + 1) * 128] for c in range(reach)], axis=0
        )
        blocks = []
        for c in range(reach):
            shape = (4 * lines, count)
            dz = (iota(shape, 1) >> line_bits) - (iota(shape, 0) >> line_bits)
            dz = dz - ((slab >> down) - 1)
            dy = (iota(shape, 1) & (lines - 1)) - (iota(shape, 0) & (lines - 1))
            squared = dz * dz + dy * dy
            if level < 5:
                weight = jnp.zeros(shape, jnp.float32)
                for value in SQUARES:
                    weight = jnp.where(
                        squared == value, level_weight(level, value + c * c), weight
                    )
                weight = jnp.where((jnp.abs(dz) <= 2) & (jnp.abs(dy) <= 2), weight, 0.0)
            else:
                weight = (1.0 / F) / jnp.sqrt((squared + (c * c + 1)).astype(jnp.float32))
            blocks.append(dot32(weight, stacked[c * count : (c + 1) * count]))
        field3[first_row : first_row + 4 * lines, :] = sum(blocks[1:], blocks[0])
        first_row = first_row + 4 * lines
        first_lane = first_lane + length

    lane = 0
    for level in range(1, 6):
        length = NX >> level
        rows = length if level < 5 else NX - lane
        weights = hat(iota((rows, NX), 1), iota((rows, NX), 0), 2**level, length)
        weights = jnp.where(iota((rows, NX), 0) < length, weights, 0.0)
        along_x[lane : lane + rows, :] = weights.astype(jnp.bfloat16)
        lane = lane + rows

    @pl.loop(0, 4)
    def _(step):

        def along_zy(level, planes, lines, plane0, line0):
            shape = (3, 48, planes * lines)
            bits = lines.bit_length() - 1
            fine_z = CZ * slab - 2 + 3 * step + iota(shape, 0)
            fine_y = CY * pencil - 8 + iota(shape, 1)
            plane = plane0 + (iota(shape, 2) >> bits)
            line = line0 + (iota(shape, 2) & (lines - 1))
            weights = hat(fine_z, plane, 2**level, (slabs * CZ) >> level) * hat(
                fine_y, line, 2**level, (pencils * CY) >> level
            )
            return weights.reshape(3 * 48, planes * lines)

        parts = [
            dot32(along_zy(1, 8, 32, 4 * slab - 2, 16 * pencil - 8), field1[...]),
            dot32(along_zy(2, 4, 32, 2 * slab - 1, 8 * pencil - 8), field2[...]),
        ]
        first_row = 0
        last = jnp.zeros((3 * 48, 128), jnp.float32)
        for level in (3, 4, 5):
            lines = (pencils * CY) >> level
            weights = along_zy(level, 4, lines, (slab >> (level - 3)) - 1, 0)
            last = last + dot32(weights, field3[first_row : first_row + 4 * lines, :])
            first_row = first_row + 4 * lines
        parts.append(last)
        high, low = split_two(jnp.concatenate(parts, axis=1))
        fine = jnp.dot(high, along_x[...], preferred_element_type=jnp.float32)
        fine += jnp.dot(low, along_x[...], preferred_element_type=jnp.float32)
        wide_pot[pl.ds(4 + 3 * step, 3)] = fine.reshape(3, 48, NX)

    for edge in (0, 1, 2, 3, 16, 17, 18, 19):
        wide_pot[edge] = jnp.zeros((48, NX), jnp.float32)

    @pl.loop(0, 16)
    def _(plane):
        values = wide0[plane]
        sums[0] = values
        sums[1] = pair_x(values, 1)
        sums[2] = pair_x(values, 2)
        for block in range(NX // 128):
            lanes = pl.ds(block * 128, 128)
            table = {}
            for c in range(3):
                part = sums[c, :, lanes]
                table[0, c] = part
                for b in (1, 2):
                    table[b, c] = pltpu.roll(part, b, 0) + pltpu.roll(part, 48 - b, 0)
            groups = {
                0: table[0, 0],
                1: table[0, 1] + table[1, 0],
                2: table[1, 1],
                4: table[0, 2] + table[2, 0],
                5: table[1, 2] + table[2, 1],
                8: table[2, 2],
            }
            for a in range(3):
                total = sum(near_weight(a * a + k) * groups[k] for k in SQUARES)
                for target in {a, -a}:
                    wide_pot[plane + 2 + target, :, lanes] += total

    @pl.loop(0, 12)
    def _(plane):
        shape = (48, NX)
        row = CY * pencil - 8 + iota(shape, 0)
        whole_plane = CZ * slab - 2 + plane + jnp.zeros(shape, jnp.int32)
        valid = (row >= 0) & (row < pencils * CY)
        valid = valid & (whole_plane >= 0) & (whole_plane < slabs * CZ)
        wide_pot[plane + 4] = jnp.where(valid, wide_pot[plane + 4], 0.0)

    def slope(after1, before1, after2, before2):
        return (8.0 * (after1 - before1) - (after2 - before2)) * (1.0 / 12.0)

    @pl.loop(0, CZ)
    def _(plane):
        middle = wide_pot[plane + 6]
        own = middle[8:40]
        pot_ref[plane] = own
        at = [wide_pot[plane + 6 + k, 8:40, :] for k in (1, -1, 2, -2)]
        across = [pltpu.roll(middle, (-k) % 48, 0)[8:40] for k in (1, -1, 2, -2)]
        along = [shift_x(own, k) for k in (1, -1, 2, -2)]
        for direction, four in enumerate((at, across, along)):
            high, low = split_two(slope(*four))
            start = pl.multiple_of(direction * ROWS + plane * CY, CY)
            high_ref[pl.ds(start, CY), :] = high
            low_ref[pl.ds(start, CY), :] = low

    atoms = cell_ref.shape[1]
    width = math.gcd(atoms, 512)

    @pl.loop(0, atoms // width)
    def _(step):
        start = pl.multiple_of(step * width, width)
        rows, columns = local_rows(cell_ref, start, width)
        charges = charge_ref[:, pl.ds(start, width)]
        at_row = iota((ROWS, width), 0) == rows
        table = jnp.where(iota((NX, width), 0) == columns, 1.0, 0.0).astype(jnp.bfloat16)
        for direction in range(3):
            part = pl.ds(direction * ROWS, ROWS)
            at_cell = jnp.dot(high_ref[part, :], table, preferred_element_type=jnp.float32)
            at_cell += jnp.dot(low_ref[part, :], table, preferred_element_type=jnp.float32)
            chosen = jnp.sum(jnp.where(at_row, at_cell, 0.0), axis=0, keepdims=True)
            force_ref[direction : direction + 1, pl.ds(start, width)] = -charges * chosen


def field_call(slabs, pencils, atom_cell, charge, wide):
    stencil1 = window_stencil(1, 12, 8, 32, -2)
    stencil2 = window_stencil(2, 10, 4, 32, -3)
    field3_rows = sum(4 * ((pencils * CY) >> level) for level in (3, 4, 5))
    return pl.pallas_call(
        functools.partial(field_kernel, slabs, pencils),
        out_shape=[
            jax.ShapeDtypeStruct((CZ, CY, NX), jnp.float32),
            jax.ShapeDtypeStruct(atom_cell.shape, jnp.float32),
        ],
        in_specs=[VMEM] * 8,
        out_specs=[VMEM] * 2,
        scratch_shapes=[
            pltpu.VMEM((3, 48, NX), jnp.float32),
            pltpu.VMEM((20, 48, NX), jnp.float32),
            pltpu.VMEM((8 * 32, NX // 2), jnp.float32),
            pltpu.VMEM((4 * 32, NX // 4), jnp.float32),
            pltpu.VMEM((field3_rows, 128), jnp.float32),
            pltpu.VMEM((NX, NX), jnp.bfloat16),
            pltpu.VMEM((3 * ROWS, NX), jnp.bfloat16),
            pltpu.VMEM((3 * ROWS, NX), jnp.bfloat16),
        ],
        compiler_params=pltpu.CompilerParams(vmem_limit_bytes=24 * 2**20),
    )(
        atom_cell,
        charge.reshape(1, -1),
        *wide,
        jnp.asarray(stencil1),
        jnp.asarray(stencil2),
    )


def solution(mesh):
    slabs = mesh.shape["slab"]
    pencils = mesh.shape["pencil"]

    def body(atom_cell, charge):
        parts = deposit_call(atom_cell, charge)
        wide = exchange_call(slabs, pencils, parts)
        potential, forces = field_call(slabs, pencils, atom_cell, charge, wide)
        return (potential, forces)

    return jax.shard_map(
        body,
        mesh=mesh,
        in_specs=(P(None, ("slab", "pencil")), P(("slab", "pencil"))),
        out_specs=(P("slab", "pencil", None), P(None, ("slab", "pencil"))),
        check_vma=False,
    )
```

```python
import functools
import math

import jax
import jax.numpy as jnp
import numpy as np
from jax import lax
from jax.experimental import pallas as pl
from jax.experimental.pallas import tpu as pltpu
from jax.sharding import PartitionSpec as P

CZ = 8
CY = 32
NX = 512
F = 32
ROWS = CZ * CY
CHUNK = 1024
MESH = pl.DeviceIdType.MESH
VMEM = pl.BlockSpec(memory_space=pltpu.VMEM)
SQUARES = (0, 1, 2, 4, 5, 8)


def iota(shape, dim):
    return lax.broadcasted_iota(jnp.int32, shape, dim)


def near_weight(squared):
    return 1.0 / math.sqrt(squared + 0.25) - 1.0 / math.sqrt(squared + 4.0)


def level_weight(level, squared):
    return (1.0 / math.sqrt(squared + 1.0) - 1.0 / math.sqrt(squared + 4.0)) / 2**level


def split_two(values):
    high = values.astype(jnp.bfloat16)
    return high, (values - high.astype(jnp.float32)).astype(jnp.bfloat16)


def dot32(left, right):
    left_high, left_low = split_two(left)
    right_high, right_low = split_two(right)
    total = jnp.dot(left_high, right_high, preferred_element_type=jnp.float32)
    total += jnp.dot(left_high, right_low, preferred_element_type=jnp.float32)
    return total + jnp.dot(left_low, right_high, preferred_element_type=jnp.float32)


def local_rows(cell_ref, start, width):
    z0 = lax.axis_index("slab") * CZ
    y0 = lax.axis_index("pencil") * CY
    plane = cell_ref[0:1, pl.ds(start, width)] - z0
    line = cell_ref[1:2, pl.ds(start, width)] - y0
    return plane * CY + line, cell_ref[2:3, pl.ds(start, width)]


def halve_rows(rows_out, rows_in, line_bits):
    out_row = iota((rows_out, rows_in), 0)
    in_row = iota((rows_out, rows_in), 1)
    plane = in_row >> (line_bits + 1)
    line = (in_row & (2**line_bits - 1)) >> 1
    return jnp.where((plane << (line_bits - 1)) + line == out_row, 1.0, 0.0)


def halve_columns(columns_in, columns_out):
    return jnp.where(
        iota((columns_in, columns_out), 0) >> 1 == iota((columns_in, columns_out), 1), 1.0, 0.0
    )


def deposit_kernel(cell_ref, charge_ref, grid_ref, one_ref, two_ref, three_ref, total_ref):
    atoms = cell_ref.shape[1]
    width = math.gcd(atoms, CHUNK)
    total_ref[...] = jnp.zeros_like(total_ref)

    @pl.loop(0, atoms // width)
    def _(step):
        start = pl.multiple_of(step * width, width)
        rows, columns = local_rows(cell_ref, start, width)
        charges = charge_ref[:, pl.ds(start, width)]
        high = charges.astype(jnp.bfloat16).astype(jnp.float32)
        low = charges - high
        at_row = iota((ROWS, width), 0) == rows
        table = jnp.where(iota((NX, width), 0) == columns, 1.0, 0.0).astype(jnp.bfloat16)
        stacked = jnp.concatenate(
            [
                jnp.where(at_row, high, 0.0).astype(jnp.bfloat16),
                jnp.where(at_row, low, 0.0).astype(jnp.bfloat16),
            ],
            axis=0,
        )
        added = lax.dot_general(
            stacked, table, (((1,), (1,)), ((), ())), preferred_element_type=jnp.float32
        )
        total_ref[...] += added[:ROWS] + added[ROWS:]

    grid = total_ref[...]
    grid_ref[...] = grid.reshape(CZ, CY, NX)
    one = dot32(dot32(halve_rows(ROWS // 4, ROWS, 5), grid), halve_columns(NX, NX // 2))
    one_ref[...] = one.reshape(CZ // 2, CY // 2, NX // 2)
    two = dot32(
        dot32(halve_rows(ROWS // 16, ROWS // 4, 4), one), halve_columns(NX // 2, NX // 4)
    )
    two_ref[...] = two.reshape(CZ // 4, CY // 4, NX // 4)
    three_ref[...] = dot32(
        dot32(halve_rows(8, ROWS // 16, 3), two), halve_columns(NX // 4, NX // 4)
    )


def deposit_call(atom_cell, charge):
    shapes = ((CZ, CY, NX), (CZ // 2, CY // 2, NX // 2), (CZ // 4, CY // 4, NX // 4), (8, 128))
    return pl.pallas_call(
        deposit_kernel,
        out_shape=[jax.ShapeDtypeStruct(shape, jnp.float32) for shape in shapes],
        in_specs=[VMEM] * 2,
        out_specs=[VMEM] * 4,
        scratch_shapes=[pltpu.VMEM((ROWS, NX), jnp.float32)],
        compiler_params=pltpu.CompilerParams(vmem_limit_bytes=48 * 2**20),
    )(atom_cell, charge.reshape(1, -1))


def window(level, dz, dy):
    if level == 0:
        z = {1: (4, 0, 4), -1: (0, 12, 4), 0: (0, 0, 16)}[dz]
        y = {1: (32, 0, 8), -1: (8, 40, 8), 0: (0, 8, 32)}[dy]
    elif level == 1:
        z = {1: (0, 0, 4), -1: (0, 8, 4), 0: (0, 0, 12)}[dz]
        y = {1: (16, 0, 8), -1: (8, 24, 8), 0: (0, 8, 16)}[dy]
    else:
        z = (0, 4 - 2 * dz, 2)
        y = (0, 8 - 8 * dy, 8)
    return z, y


def exchange_kernel(
    slabs, pencils, zero, one, two, three, wide0, wide1, wide2, wide3, send, recv, send3, recv3
):
    slab = lax.axis_index("slab")
    pencil = lax.axis_index("pencil")
    devices = slabs * pencils
    me = slab * pencils + pencil
    for ref in (wide0, wide1, wide2):
        ref[...] = jnp.zeros_like(ref)
    wide0[4:12, 8:40, :] = zero[...]
    wide1[4:8, 8:24, :] = one[...]
    wide2[4:6, 8:16, :] = two[...]
    wide3[pl.ds(me, 1)] = three[...][None]

    def place(step):
        other = lax.rem(me + step, devices)
        return (other // pencils, lax.rem(other, pencils))

    barrier = pltpu.get_barrier_semaphore()

    @pl.loop(1, devices)
    def _(step):
        pl.semaphore_signal(barrier, inc=1, device_id=place(step), device_id_type=MESH)

    pl.semaphore_wait(barrier, devices - 1)

    offsets = [(level, dz, 0) for level in (0, 1) for dz in (-1, 1)]
    offsets += [(level, 0, dy) for level in (0, 1) for dy in (-1, 1)]
    offsets += [(2, dz, dy) for dz in range(-2, 3) for dy in (-1, 0, 1) if dz or dy]
    sources = (zero, one, two)
    targets = (wide0, wide1, wide2)

    def inside(dz, dy):
        z = slab + dz
        y = pencil + dy
        return (z >= 0) & (z < slabs) & (y >= 0) & (y < pencils)

    def copy_of(index, device):
        level, dz, dy = offsets[index]
        (zs, zd, zn), (ys, yd, yn) = window(level, dz, dy)
        return pltpu.make_async_remote_copy(
            src_ref=(targets if level < 2 and dy else sources)[level].at[pl.ds(zs, zn), pl.ds(ys, yn), :],
            dst_ref=targets[level].at[pl.ds(zd, zn), pl.ds(yd, yn), :],
            send_sem=send.at[index],
            recv_sem=recv.at[index],
            device_id=device,
            device_id_type=MESH,
        )

    def top_copy(step, slot):
        return pltpu.make_async_remote_copy(
            src_ref=three,
            dst_ref=wide3.at[slot],
            send_sem=send3.at[step],
            recv_sem=recv3.at[step],
            device_id=place(step),
            device_id_type=MESH,
        )

    def start(indices):
        for index in indices:
            level, dz, dy = offsets[index]

            @pl.when(inside(dz, dy))
            def _(index=index, dz=dz, dy=dy):
                copy_of(index, (slab + dz, pencil + dy)).start()

    def finish(indices):
        for index in indices:
            level, dz, dy = offsets[index]

            @pl.when(inside(-dz, -dy))
            def _(index=index, dz=dz, dy=dy):
                copy_of(index, (slab - dz, pencil - dy)).wait_recv()

            @pl.when(inside(dz, dy))
            def _(index=index, dz=dz, dy=dy):
                copy_of(index, (slab + dz, pencil + dy)).wait_send()

    start(range(4))
    start(range(8, len(offsets)))

    @pl.loop(1, devices)
    def _(step):
        top_copy(step, me).start()

    finish(range(4))
    start(range(4, 8))

    @pl.loop(1, devices)
    def _(step):
        copy = top_copy(step, lax.rem(me + devices - step, devices))
        copy.wait_send()
        copy.wait_recv()

    finish(range(4, len(offsets)))


def exchange_call(slabs, pencils, parts):
    devices = slabs * pencils
    shapes = ((16, 48, NX), (12, 32, NX // 2), (10, 32, NX // 4), (devices, 8, 128))
    return pl.pallas_call(
        functools.partial(exchange_kernel, slabs, pencils),
        out_shape=[jax.ShapeDtypeStruct(shape, jnp.float32) for shape in shapes],
        in_specs=[VMEM] * 4,
        out_specs=[VMEM] * 4,
        scratch_shapes=[
            pltpu.SemaphoreType.DMA((22,)),
            pltpu.SemaphoreType.DMA((22,)),
            pltpu.SemaphoreType.DMA((devices,)),
            pltpu.SemaphoreType.DMA((devices,)),
        ],
        compiler_params=pltpu.CompilerParams(
            collective_id=0, has_side_effects=True, vmem_limit_bytes=48 * 2**20
        ),
    )(*parts)


def shift_x(values, step):
    width = values.shape[-1]
    axis = values.ndim - 1
    column = iota(values.shape, axis)
    moved = pltpu.roll(values, (-step) % width, axis)
    return jnp.where((column + step >= 0) & (column + step < width), moved, 0.0)


def pair_x(values, step):
    return shift_x(values, step) + shift_x(values, -step)


def hat(fine, cell, factor, count):
    bits = factor.bit_length()
    numerator = jnp.clip(2 * fine + 1 - factor, 0, 2 * factor * (count - 1))
    lower = jnp.minimum(numerator >> bits, count - 2)
    fraction = (numerator - (lower << bits)).astype(jnp.float32) * (0.5 / factor)
    return jnp.where(
        cell == lower, 1.0 - fraction, jnp.where(cell == lower + 1, fraction, 0.0)
    )


def window_stencil(level, planes_in, planes_out, lines, shift):
    blocks = []
    dz = np.arange(planes_in)[None, :] - np.arange(planes_out)[:, None] + shift
    dy = np.arange(lines)[None, :] - np.arange(lines)[:, None]
    dz = dz[:, None, :, None]
    dy = dy[None, :, None, :]
    near = (np.abs(dz) <= 2) & (np.abs(dy) <= 2)
    for c in range(3):
        squared = (dz * dz + dy * dy + c * c).astype(np.float64)
        weight = (1.0 / np.sqrt(squared + 1.0) - 1.0 / np.sqrt(squared + 4.0)) / 2**level
        weight = np.where(near, weight, 0.0)
        blocks.append(weight.reshape(planes_out * lines, planes_in * lines))
    return np.concatenate(blocks, axis=1).astype(np.float32)


def field_kernel(
    slabs,
    pencils,
    cell_ref,
    charge_ref,
    wide0,
    wide1,
    wide2,
    wide3,
    stencil1,
    stencil2,
    pot_ref,
    force_ref,
    sums,
    wide_pot,
    field1,
    field2,
    field3,
    along_x,
    high_ref,
    low_ref,
):
    slab = lax.axis_index("slab")
    pencil = lax.axis_index("pencil")
    pencil_bits = pencils.bit_length() - 1

    grid1 = wide1[...].reshape(12 * 32, NX // 2)
    field1[...] = dot32(
        stencil1[...], jnp.concatenate([grid1, pair_x(grid1, 1), pair_x(grid1, 2)], axis=0)
    )
    grid2 = wide2[...].reshape(10 * 32, NX // 4)
    field2[...] = dot32(
        stencil2[...], jnp.concatenate([grid2, pair_x(grid2, 1), pair_x(grid2, 2)], axis=0)
    )
    rows3 = slabs * pencils * 8
    grid3 = wide3[...].reshape(rows3, 128)
    coarse = []
    first_row = 0
    first_lane = 0
    for level in (3, 4, 5):
        down = level - 3
        line_bits = pencil_bits + 2 - down
        lines = 2**line_bits
        planes = slabs >> down
        count = planes * lines
        length = NX >> level
        shape = (count, rows3)
        out_row = iota(shape, 0)
        in_row = iota(shape, 1)
        in_plane = in_row >> (3 + pencil_bits)
        in_line = (((in_row >> 3) & (pencils - 1)) << 2) + (in_row & 7)
        cell = ((in_plane >> down) << line_bits) + (in_line >> down)
        chosen = jnp.where((cell == out_row) & ((in_row & 7) < 4), 1.0, 0.0)
        charges = dot32(chosen, grid3)
        reach = 3 if level < 5 else length
        source = iota((128, 128), 0) >> down
        column = iota((128, 128), 1) - first_lane
        valid = (column >= 0) & (column < length)
        pairs = jnp.concatenate(
            [
                jnp.where(valid & (jnp.abs(source - column) == c), 1.0, 0.0)
                for c in range(reach)
            ],
            axis=1,
        )
        moved = dot32(charges, pairs)
        stacked = jnp.concatenate(
            [moved[:, c * 128 : (c + 1) * 128] for c in range(reach)], axis=0
        )
        blocks = []
        for c in range(reach):
            shape = (4 * lines, count)
            dz = (iota(shape, 1) >> line_bits) - (iota(shape, 0) >> line_bits)
            dz = dz - ((slab >> down) - 1)
            dy = (iota(shape, 1) & (lines - 1)) - (iota(shape, 0) & (lines - 1))
            squared = dz * dz + dy * dy
            if level < 5:
                weight = jnp.zeros(shape, jnp.float32)
                for value in SQUARES:
                    weight = jnp.where(
                        squared == value, level_weight(level, value + c * c), weight
                    )
                weight = jnp.where((jnp.abs(dz) <= 2) & (jnp.abs(dy) <= 2), weight, 0.0)
            else:
                weight = (1.0 / F) / jnp.sqrt((squared + (c * c + 1)).astype(jnp.float32))
            blocks.append(dot32(weight, stacked[c * count : (c + 1) * count]))
        field3[first_row : first_row + 4 * lines, :] = sum(blocks[1:], blocks[0])
        first_row = first_row + 4 * lines
        first_lane = first_lane + length

    lane = 0
    for level in range(1, 6):
        length = NX >> level
        rows = length if level < 5 else NX - lane
        weights = hat(iota((rows, NX), 1), iota((rows, NX), 0), 2**level, length)
        weights = jnp.where(iota((rows, NX), 0) < length, weights, 0.0)
        along_x[lane : lane + rows, :] = weights.astype(jnp.bfloat16)
        lane = lane + rows

    @pl.loop(0, 4)
    def _(step):

        def along_zy(level, planes, lines, plane0, line0):
            shape = (3, 48, planes * lines)
            bits = lines.bit_length() - 1
            fine_z = CZ * slab - 2 + 3 * step + iota(shape, 0)
            fine_y = CY * pencil - 8 + iota(shape, 1)
            plane = plane0 + (iota(shape, 2) >> bits)
            line = line0 + (iota(shape, 2) & (lines - 1))
            weights = hat(fine_z, plane, 2**level, (slabs * CZ) >> level) * hat(
                fine_y, line, 2**level, (pencils * CY) >> level
            )
            return weights.reshape(3 * 48, planes * lines)

        parts = [
            dot32(along_zy(1, 8, 32, 4 * slab - 2, 16 * pencil - 8), field1[...]),
            dot32(along_zy(2, 4, 32, 2 * slab - 1, 8 * pencil - 8), field2[...]),
        ]
        first_row = 0
        last = jnp.zeros((3 * 48, 128), jnp.float32)
        for level in (3, 4, 5):
            lines = (pencils * CY) >> level
            weights = along_zy(level, 4, lines, (slab >> (level - 3)) - 1, 0)
            last = last + dot32(weights, field3[first_row : first_row + 4 * lines, :])
            first_row = first_row + 4 * lines
        parts.append(last)
        high, low = split_two(jnp.concatenate(parts, axis=1))
        fine = jnp.dot(high, along_x[...], preferred_element_type=jnp.float32)
        fine += jnp.dot(low, along_x[...], preferred_element_type=jnp.float32)
        wide_pot[pl.ds(4 + 3 * step, 3)] = fine.reshape(3, 48, NX)

    for edge in (0, 1, 2, 3, 16, 17, 18, 19):
        wide_pot[edge] = jnp.zeros((48, NX), jnp.float32)

    @pl.loop(0, 16)
    def _(plane):
        values = wide0[plane]
        sums[0] = values
        sums[1] = pair_x(values, 1)
        sums[2] = pair_x(values, 2)
        for block in range(NX // 128):
            lanes = pl.ds(block * 128, 128)
            table = {}
            for c in range(3):
                part = sums[c, :, lanes]
                table[0, c] = part
                for b in (1, 2):
                    table[b, c] = pltpu.roll(part, b, 0) + pltpu.roll(part, 48 - b, 0)
            groups = {
                0: table[0, 0],
                1: table[0, 1] + table[1, 0],
                2: table[1, 1],
                4: table[0, 2] + table[2, 0],
                5: table[1, 2] + table[2, 1],
                8: table[2, 2],
            }
            for a in range(3):
                total = sum(near_weight(a * a + k) * groups[k] for k in SQUARES)
                for target in {a, -a}:
                    wide_pot[plane + 2 + target, :, lanes] += total

    @pl.loop(0, 12)
    def _(plane):
        shape = (48, NX)
        row = CY * pencil - 8 + iota(shape, 0)
        whole_plane = CZ * slab - 2 + plane + jnp.zeros(shape, jnp.int32)
        valid = (row >= 0) & (row < pencils * CY)
        valid = valid & (whole_plane >= 0) & (whole_plane < slabs * CZ)
        wide_pot[plane + 4] = jnp.where(valid, wide_pot[plane + 4], 0.0)

    def slope(after1, before1, after2, before2):
        return (8.0 * (after1 - before1) - (after2 - before2)) * (1.0 / 12.0)

    @pl.loop(0, CZ)
    def _(plane):
        middle = wide_pot[plane + 6]
        own = middle[8:40]
        pot_ref[plane] = own
        at = [wide_pot[plane + 6 + k, 8:40, :] for k in (1, -1, 2, -2)]
        across = [pltpu.roll(middle, (-k) % 48, 0)[8:40] for k in (1, -1, 2, -2)]
        along = [shift_x(own, k) for k in (1, -1, 2, -2)]
        for direction, four in enumerate((at, across, along)):
            high, low = split_two(slope(*four))
            start = pl.multiple_of(direction * ROWS + plane * CY, CY)
            high_ref[pl.ds(start, CY), :] = high
            low_ref[pl.ds(start, CY), :] = low

    atoms = cell_ref.shape[1]
    width = math.gcd(atoms, 512)

    @pl.loop(0, atoms // width)
    def _(step):
        start = pl.multiple_of(step * width, width)
        rows, columns = local_rows(cell_ref, start, width)
        charges = charge_ref[:, pl.ds(start, width)]
        at_row = iota((ROWS, width), 0) == rows
        table = jnp.where(iota((NX, width), 0) == columns, 1.0, 0.0).astype(jnp.bfloat16)
        for direction in range(3):
            part = pl.ds(direction * ROWS, ROWS)
            at_cell = jnp.dot(high_ref[part, :], table, preferred_element_type=jnp.float32)
            at_cell += jnp.dot(low_ref[part, :], table, preferred_element_type=jnp.float32)
            chosen = jnp.sum(jnp.where(at_row, at_cell, 0.0), axis=0, keepdims=True)
            force_ref[direction : direction + 1, pl.ds(start, width)] = -charges * chosen


def field_call(slabs, pencils, atom_cell, charge, wide):
    stencil1 = window_stencil(1, 12, 8, 32, -2)
    stencil2 = window_stencil(2, 10, 4, 32, -3)
    field3_rows = sum(4 * ((pencils * CY) >> level) for level in (3, 4, 5))
    return pl.pallas_call(
        functools.partial(field_kernel, slabs, pencils),
        out_shape=[
            jax.ShapeDtypeStruct((CZ, CY, NX), jnp.float32),
            jax.ShapeDtypeStruct(atom_cell.shape, jnp.float32),
        ],
        in_specs=[VMEM] * 8,
        out_specs=[VMEM] * 2,
        scratch_shapes=[
            pltpu.VMEM((3, 48, NX), jnp.float32),
            pltpu.VMEM((20, 48, NX), jnp.float32),
            pltpu.VMEM((8 * 32, NX // 2), jnp.float32),
            pltpu.VMEM((4 * 32, NX // 4), jnp.float32),
            pltpu.VMEM((field3_rows, 128), jnp.float32),
            pltpu.VMEM((NX, NX), jnp.bfloat16),
            pltpu.VMEM((3 * ROWS, NX), jnp.bfloat16),
            pltpu.VMEM((3 * ROWS, NX), jnp.bfloat16),
        ],
        compiler_params=pltpu.CompilerParams(vmem_limit_bytes=24 * 2**20),
    )(
        atom_cell,
        charge.reshape(1, -1),
        *wide,
        jnp.asarray(stencil1),
        jnp.asarray(stencil2),
    )


def solution(mesh):
    slabs = mesh.shape["slab"]
    pencils = mesh.shape["pencil"]

    def body(atom_cell, charge):
        parts = deposit_call(atom_cell, charge)
        wide = exchange_call(slabs, pencils, parts)
        potential, forces = field_call(slabs, pencils, atom_cell, charge, wide)
        return (potential, forces)

    return jax.shard_map(
        body,
        mesh=mesh,
        in_specs=(P(None, ("slab", "pencil")), P(("slab", "pencil"))),
        out_specs=(P("slab", "pencil", None), P(None, ("slab", "pencil"))),
        check_vma=False,
    )
```
